32 devices in a mesh: shots: 2 (over y), freq: 4 (over x, core), tile: 4 (over z).
Axes of the slice: x: 2, y: 2, z: 4, core: 2. Of those that a mesh axis runs over, the one named last changes fastest.
Arguments:
- velocity: float32 [4, 96, 1024], P(None, 'tile', 'freq'), may hold values from 1.5 to 4.5
- src_cell: int32 [8192], P('shots'), parts along dimension 0, may hold values from 0 to 98303
- src_wave: float32 [2, 4, 8192], P(None, 'freq', 'shots'), parts along dimension 2, may hold values from -24 to 24
- rec_cell: int32 [32768], P('shots'), parts along dimension 0, may hold values from 0 to 98303
- rec_data: float32 [2, 4, 32768], P(None, 'freq', 'shots'), parts along dimension 2, may hold values from -24 to 24
Outputs:
- final_fields: float32 [4, 4, 2, 96, 1024], P('shots', 'freq', None, 'tile'), parts along dimension 0
- migrated_image: float32 [8, 96, 1024], P('shots', 'tile', 'freq'), parts along dimension 0
The draws below stay inside these ranges and needn't reach their ends.
There are 2 independent parts, one for each index of `shots`. The reference program is written for one: setup_inputs(seed, part) draws one part's arguments, and reference() takes and returns one part's arrays. A program takes and returns all parts, laid end to end along the dimension named above; an argument that names none is the same for every part. Nothing has to cross between parts.
Inputs may be any that keep to these rules, and one draw needn't show every extreme that they name: `src_cell`: each entry is a surface cell numbered row * 1024 + column; cells may repeat. `rec_cell`: each entry is a surface cell numbered row * 1024 + column; cells may repeat.
All inputs are finite; a program needn't handle non-finite values.
Results may differ from the reference program's by a relative error of at most 0.00002.
Values sent between devices are 32-bit elements; how exact they have to be, the bound alone decides.
No kernel may reach another device: no remote copies, remote signals or barrier semaphores. Data moves between devices by JAX's collectives and lax.ppermute only.
A program may use at most 128 MiB of HBM per device.

```python
import math
import jax
import jax.numpy as jnp
from jax import lax

NY = 1024
STEPS = 4
PASSES = 5
NSRC = 4096
NREC = 16384
NX = 96
FREQS = 4


def set_ends(entries, own_key, low, top_value):
    extent = entries.shape
    index_at = [jax.random.randint(jax.random.fold_in(own_key, axis), (), 0, extent[axis]) for axis in range(len(extent))]
    entries = entries.at[tuple(index_at)].set(low)
    longest = extent.index(max(extent))
    index_at[longest] = (index_at[longest] + 1) % extent[longest]
    return entries.at[tuple(index_at)].set(top_value)


def block_scale(rng, dims, cuts, least, largest):
    def one(dim, parts):
        heights = jax.random.uniform(jax.random.fold_in(jax.random.fold_in(rng, 6), dim), (parts,), jnp.float32, least / len(cuts), largest / len(cuts))
        return jnp.repeat(jnp.exp(heights), dims[dim] // parts).reshape((-1,) + (1,) * (len(dims) - dim - 1))

    loudness = one(*cuts[0])
    for cut in cuts[1:]:
        loudness = loudness * one(*cut)
    return loudness


def noise(key, extent, scale, limit, pieces=(), kind=jnp.bfloat16):
    level = block_scale(key, extent, pieces, -0.22, 0.18) if pieces else 1.0
    drawn = jax.random.normal(key, extent, jnp.float32) * scale * level
    return jnp.minimum(jnp.maximum(drawn, -limit), limit).astype(kind)


def setup_inputs(seed: int = 0, part: int = 0) -> dict:
    arg_keys = jax.random.split(jax.random.key(seed), 6)
    part_splits = jax.random.split(jax.random.fold_in(arg_keys[5], part), 6)
    return {
        "velocity": jnp.clip(jnp.exp(math.log(4.5) - 1.0986123 * jax.random.uniform(arg_keys[0], (STEPS, NX, NY), jnp.float32) ** block_scale(arg_keys[0], (STEPS, NX, NY), ((1, 4), (2, 4)), -0.2, 0.2)), 1.5, 4.5),
        "src_cell": set_ends(jax.random.randint(part_splits[1], (NSRC,), 0, NX * NY), jax.random.fold_in(part_splits[1], 1), 0, (NX * NY) - 1).astype(jnp.int32),
        "src_wave": noise(part_splits[2], (2, FREQS, NSRC), 4.0, 24.0, ((1, 4),), jnp.float32),
        "rec_cell": set_ends(jax.random.randint(part_splits[3], (NREC,), 0, NX * NY), jax.random.fold_in(part_splits[3], 1), 0, (NX * NY) - 1).astype(jnp.int32),
        "rec_data": noise(part_splits[4], (2, FREQS, NREC), 4.0, 24.0, ((1, 4),), jnp.float32),
    }


term_weights = (0.30, 0.25, -0.15, 0.12, -0.10, 0.08)
phase_rates = (1.0, 0.8, 0.6, 0.45, 0.3, 0.2)
phase_unit = 0.25


def along_cols(values):
    blank_edge = jnp.zeros_like(values[..., :1])
    return jnp.concatenate([values[..., 1:], blank_edge], axis=-1) + jnp.concatenate([blank_edge, values[..., :-1]], axis=-1)


def mcclellan(padded):
    center = padded[..., 1:-1, :]
    across = padded[..., 2:, :] + padded[..., :-2, :]
    return -0.5 * center + 0.25 * across + 0.25 * along_cols(center) + 0.125 * along_cols(across)


def weighted(term, term_order, phase_base, conj_sign):
    real_coef = term_weights[term_order] * jnp.cos(phase_rates[term_order] * phase_base)
    imag_coef = conj_sign * (term_weights[term_order] * jnp.sin(phase_rates[term_order] * phase_base))
    term_real = term[..., 0, :, :]
    term_imag = term[..., 1, :, :]
    return jnp.stack([real_coef * term_real - imag_coef * term_imag, real_coef * term_imag + imag_coef * term_real], axis=-3)


def pad_rows(values):
    widths = [(0, 0)] * (values.ndim - 2) + [(1, 1), (0, 0)]
    return jnp.pad(values, widths)


def extrapolate(fields, phase_base, conj_sign):
    previous = fields
    summed = weighted(previous, 0, phase_base, conj_sign)
    current = mcclellan(pad_rows(previous))
    summed = summed + weighted(current, 1, phase_base, conj_sign)
    for term_order in range(2, PASSES + 1):
        following = 2.0 * mcclellan(pad_rows(current)) - previous
        summed = summed + weighted(following, term_order, phase_base, conj_sign)
        previous, current = current, following
    return summed


def inject(cell_ids, spectra):
    flat_field = jnp.zeros((2, NX * NY), jnp.float32).at[:, cell_ids].add(spectra)
    return flat_field.reshape(2, NX, NY)


def reference(velocity, src_cell, src_wave, rec_cell, rec_data):
    conj_sign = jnp.array([1.0, -1.0], jnp.float32).reshape(2, 1, 1)

    def one_frequency(image_sum, freq_index):
        fields = jnp.stack([inject(src_cell, src_wave[:, freq_index, :]), inject(rec_cell, rec_data[:, freq_index, :])])
        number = (freq_index + 1).astype(jnp.float32)
        depth_images = []
        for depth_step in range(STEPS):
            phase_base = number * phase_unit / velocity[depth_step]
            fields = extrapolate(fields, phase_base, conj_sign)
            depth_images.append(fields[0, 0] * fields[1, 0] + fields[0, 1] * fields[1, 1])
        return image_sum + jnp.stack(depth_images), fields

    empty_image = jnp.zeros((STEPS, NX, NY), jnp.float32)
    migrated_image, stacked = lax.scan(one_frequency, empty_image, jnp.arange(FREQS, dtype=jnp.int32))
    return jnp.transpose(stacked, (1, 0, 2, 3, 4)), migrated_image
```

```python
import functools

import jax
import jax.numpy as jnp
from jax import lax
from jax.experimental import pallas as pl
from jax.experimental.pallas import tpu as pltpu
from jax.sharding import PartitionSpec as P

PASSES = 5
LANES = 128
SUB = 8
CHUNK = 1024
UNROLL = 4
BLOCK = 256

term_weights = (0.3, 0.25, -0.15, 0.12, -0.1, 0.08)
phase_unit = 0.25
slowest = 1.5


def round_up(value, unit):
    return -(-value // unit) * unit


def inject_kernel(rows, halo, row_count, cell_ref, wave_ref, out_ref):
    chunk = min(CHUNK, cell_ref.shape[0] * LANES)
    chunks = cell_ref.shape[0] * LANES // chunk
    blocks = out_ref.shape[1] // 2
    pair = 2 * LANES
    cols = blocks * pair
    high_count = blocks * rows
    tall = 2 * SUB
    first = lax.axis_index("tile") * row_count - halo
    size = min(BLOCK, max(high_count, pair))
    ids = lax.broadcasted_iota(jnp.int32, (size, LANES), 0).astype(jnp.float32).astype(jnp.bfloat16)

    def spread(values, line, count):
        one = jnp.broadcast_to(values[line : line + 1], (tall, LANES)).astype(jnp.bfloat16)
        return jnp.concatenate([one] * (count // tall), axis=0)

    def one_hot(index, line, count):
        return jnp.maximum(1.0 - jnp.abs(ids[:count] - spread(index, line, count)), 0.0)

    def add(index):
        lines = chunk // LANES
        lefts, rights = [], []
        for group in range(0, lines, SUB):
            height = min(SUB, lines)
            at = pl.ds(pl.multiple_of(index * lines + group, height), height)
            cell = cell_ref[at, :]
            row = cell // cols - first
            col = cell % cols
            high = jnp.where((row >= 0) & (row < rows), col // pair * rows + row, -1)
            low = ((col % 2) * LANES + col % pair // 2).astype(jnp.float32)
            pieces = []
            for part in range(2):
                value = wave_ref[part, at, :]
                top = value.astype(jnp.bfloat16).astype(jnp.float32)
                pieces += [top, value - top]
            for line in range(height):
                rights.append(one_hot(low, line, pair))
                variants = [[] for _ in pieces]
                for base in range(0, high_count, size):
                    count = min(size, high_count - base)
                    match = one_hot((high - base).astype(jnp.float32), line, count)
                    for variant, piece in zip(variants, pieces):
                        variant.append(match * spread(piece, line, count))
                lefts.append(jnp.concatenate(sum(variants, []), axis=0))
        total = lax.dot_general(
            jnp.concatenate(lefts, axis=1),
            jnp.concatenate(rights, axis=1),
            (((1,), (1,)), ((), ())),
            preferred_element_type=jnp.float32,
        )
        for part in range(2):
            at = 2 * part * high_count
            both = total[at : at + high_count] + total[at + high_count : at + 2 * high_count]
            for odd in range(2):
                out_at = slice(odd * blocks, (odd + 1) * blocks)
                out_ref[part, out_at] = out_ref[part, out_at] + both[:, odd * LANES : (odd + 1) * LANES].reshape(
                    blocks, rows, LANES
                )

    out_ref[...] = jnp.zeros_like(out_ref)
    unroll = next(u for u in (UNROLL, 2, 1) if chunks % u == 0)

    def some_chunks(index, carry):
        for one in range(unroll):
            add(index * unroll + one)
        return carry

    lax.fori_loop(0, chunks // unroll, some_chunks, 0)


def inject(cells, waves, rows, halo, row_count, cols):
    points = cells.shape[0]
    whole = pl.BlockSpec(memory_space=pltpu.VMEM)
    return pl.pallas_call(
        functools.partial(inject_kernel, rows, halo, row_count),
        out_shape=jax.ShapeDtypeStruct((2, cols // LANES, rows, LANES), jnp.float32),
        in_specs=[whole, whole],
        out_specs=whole,
        cost_estimate=pl.CostEstimate(
            flops=8 * rows * cols * points, bytes_accessed=12 * points, transcendentals=0
        ),
        name="inject",
    )(cells.reshape(points // LANES, LANES), waves.reshape(2, points // LANES, LANES))


def sine(angle, square, terms):
    total = None
    for k in range(terms - 1, 0, -1):
        coef = 1.0
        for m in range(2, 2 * k + 2):
            coef /= m
        coef = coef if k % 2 == 0 else -coef
        total = coef if total is None else total * square + coef
    return angle * (total * square + 1.0)


def cosine(square, terms):
    total = None
    for k in range(terms - 1, 0, -1):
        coef = 1.0
        for m in range(2, 2 * k + 1):
            coef /= m
        coef = coef if k % 2 == 0 else -coef
        total = coef if total is None else total * square + coef
    return total * square + 1.0


def terms_for(largest, offset):
    count, size = 1, largest * largest / ((1 + offset) * (2 + offset))
    while size > 3e-8 or count < 2:
        count += 1
        size *= largest * largest / ((2 * count - 1 + offset) * (2 * count + offset))
    return count


def times(a, b):
    return a[0] * b[0] - a[1] * b[1], a[0] * b[1] + a[1] * b[0]


def squared(a):
    twice = a[1] + a[1]
    return 1.0 - twice * a[1], twice * a[0]


def coefficients(speed, number, limit):
    slow = (0.2 * phase_unit) * number / jnp.maximum(speed, 1.0)
    square = slow * slow
    sines, cosines = terms_for(0.2 * limit, 1), terms_for(0.2 * limit, 0)
    a20 = (cosine(square, cosines), sine(slow, square, sines))
    small, square = slow * 0.75, square * 0.5625
    a15 = (cosine(square, cosines), sine(small, square, sines))
    a30 = squared(a15)
    a45 = times(a30, a15)
    a60 = squared(a30)
    a80 = times(a60, a20)
    a100 = times(a80, a20)
    angles = (a100, a80, a60, a45, a30, a20)
    return [(weight * a[0], weight * a[1]) for weight, a in zip(term_weights, angles)]


def depth_kernel(sizes, *refs):
    row_count, steps, halo, vel_halo = sizes
    freqs = lax.axis_size("freq")
    tiles = lax.axis_size("tile")
    pieces, (before_ref, after_ref, src_ref, rec_ref) = refs[:freqs], refs[freqs : freqs + 4]
    fields_ref, *image_refs = refs[freqs + 4 : 2 * freqs + 5]
    terms, sums, speed, flat, sem = refs[2 * freqs + 5 :]
    me = lax.axis_index("freq")
    tile = lax.axis_index("tile")
    number = (me + 1).astype(jnp.float32)
    limit = freqs * phase_unit / slowest
    rows = row_count + 2 * halo
    parts = src_ref.shape[1]
    blocks = parts // 2
    width = pieces[0].shape[-1]
    per_owner = width // LANES

    pending = []

    def copy(src, dst):
        pending.append(pltpu.make_async_copy(src, dst, sem.at[copy.started]))
        pending[-1].start()
        copy.started += 1

    def finish():
        while pending:
            pending.pop(0).wait()

    copy.started = 0
    for field, ref in enumerate((src_ref, rec_ref)):
        for part in range(2):
            copy(ref.at[part], terms.at[0, 2 * field + part, :, :rows, :])
    arrived = pending[:]
    for back, piece in enumerate(pieces):
        owner = lax.rem(me + freqs - back, freqs)
        for part in range(per_owner):
            lanes = slice(part * LANES, (part + 1) * LANES)
            for ref, low, size in (
                (piece, vel_halo, row_count),
                (before_ref.at[back], 0, vel_halo),
                (after_ref.at[back], vel_halo + row_count, vel_halo),
            ):
                copy(ref.at[:, :, lanes], speed.at[:, owner * per_owner + part, low : low + size, :])

    shape = (SUB, LANES)
    lane = lax.broadcasted_iota(jnp.int32, shape, 1)
    sub = lax.broadcasted_iota(jnp.int32, shape, 0)
    first_lane, last_lane = lane == 0, lane == LANES - 1
    zero = jnp.zeros(shape, jnp.float32)
    edges = (
        (halo - 1, jnp.where(tile == 0, 0.0, 1.0)),
        (halo + row_count, jnp.where(tile == tiles - 1, 0.0, 1.0)),
    )

    def strided(low, count, index=0):
        return pl.ds(low + index, SUB, stride=count)

    def take(value, index):
        return jnp.take_along_axis(value, index, axis=1, mode="promise_in_bounds")

    def split(low, high):
        index = (2 * lane) % LANES
        return [
            jnp.where(lane < LANES // 2, take(low, index + odd), take(high, index + odd)) for odd in range(2)
        ]

    def join(even, odd):
        index = lane // 2
        return [
            jnp.where(lane % 2 == 1, take(odd, index + at), take(even, index + at)) for at in (0, LANES // 2)
        ]

    def share(low, high):
        count = -(-(high - low) // SUB)
        return count + (count % SUB == 0)

    for one in arrived:
        one.wait()
        pending.remove(one)

    def one_pass(order, low, high):
        count = share(low, high)
        keeps = {}
        for row, keep in edges:
            at, index = divmod(row - low, count)
            if 0 <= at < SUB:
                keeps.setdefault(index, []).append(jnp.where(sub == at, keep, 1.0))

        def plane_body(plane, carry):
            def load(part, index):
                return terms[order - 1, plane, part, strided(low, count, index), :]

            here = [load(part, 0) for part in range(parts)]
            pair = [load(part, -1) + here[part] for part in range(parts)]
            for index in range(count):
                below = [load(part, index + 1) for part in range(parts)]
                next_pair = [here[part] + below[part] for part in range(parts)]
                stacked = [pair[part] + next_pair[part] for part in range(parts)]
                moved = [pltpu.roll(v, LANES - 1 if part < blocks else 1, 1) for part, v in enumerate(stacked)]
                for part in range(parts):
                    blk = part % blocks
                    even, odd = stacked[blk], stacked[blocks + blk]
                    if part < blocks:
                        other = moved[part + blocks - 1] if blk > 0 else zero
                        side = jnp.where(first_lane, other, moved[part + blocks])
                        total = (even + odd) + even + side
                    else:
                        other = moved[blk + 1] if blk + 1 < blocks else zero
                        side = jnp.where(last_lane, other, moved[blk])
                        total = (even + odd) + odd + side
                    at = strided(low, count, index)
                    if order == 1:
                        total = 0.125 * total
                    else:
                        total = 0.25 * total - sums[plane, part, at, :]
                    new = total - here[part]
                    for keep in keeps.get(index, []):
                        new = new * keep
                        total = total * keep
                    if order < PASSES:
                        sums[plane, part, at, :] = total
                    terms[order, plane, part, at, :] = new
                here, pair = below, next_pair
            return carry

        lax.fori_loop(0, 4, plane_body, 0)

    def put(slot, blk, at, pair):
        for half, value in enumerate(join(*pair)):
            flat[slot, 2 * blk + half, at, :] = value

    for step in range(steps):
        for order in range(1, PASSES + 1):
            one_pass(order, PASSES * step + order, rows - PASSES * step - order)
        low, high = PASSES * (step + 1), rows - PASSES * (step + 1)
        count = share(low, high)
        last = step == steps - 1
        if step == 0:
            finish()

        def blend(index, carry):
            at = strided(low, count, index)
            vel_at = strided(low - halo + vel_halo, count, index)
            for blk in range(blocks):
                done = []
                speeds = split(*[speed[step, 2 * blk + half, vel_at, :] for half in range(2)])
                for odd in range(2):
                    part = odd * blocks + blk
                    coefs = coefficients(speeds[odd], number, limit)
                    results = []
                    for field in range(2):
                        real, imag = [], []
                        for order, (cr, ci) in enumerate(coefs):
                            tr = terms[order, 2 * field, part, at, :]
                            ti = terms[order, 2 * field + 1, part, at, :]
                            if field == 0:
                                real += [cr * tr - ci * ti]
                                imag += [cr * ti + ci * tr]
                            else:
                                real += [cr * tr + ci * ti]
                                imag += [cr * ti - ci * tr]
                        results += [sum(real[1:], real[0]), sum(imag[1:], imag[0])]
                    if last:
                        results.append(results[0] * results[2] + results[1] * results[3])
                    else:
                        for plane in range(4):
                            terms[0, plane, part, at, :] = results[plane]
                    done.append(results)
                if last:
                    out_at = strided(0, count, index)
                    for slot, pair in zip((0, 1, 2, 3, 4 + step), zip(*done)):
                        put(slot, blk, out_at, pair)
            return carry

        lax.fori_loop(0, count, blend, 0)
        if not last:
            image_count = row_count // SUB

            def correlate(index, carry):
                for blk in range(blocks):
                    pair = []
                    for odd in range(2):
                        field = [
                            terms[0, plane, odd * blocks + blk, strided(halo, image_count, index), :]
                            for plane in range(4)
                        ]
                        pair.append(field[0] * field[2] + field[1] * field[3])
                    put(4 + step, blk, strided(0, image_count, index), pair)
                return carry

            lax.fori_loop(0, image_count, correlate, 0)

        for ahead, ref in enumerate(image_refs):
            owner = lax.rem(me + ahead, freqs)
            for part in range(per_owner):
                lanes = slice(part * LANES, (part + 1) * LANES)
                copy(flat.at[4 + step, owner * per_owner + part], ref.at[step, :, lanes])
    for plane in range(4):
        for part in range(parts):
            lanes = slice(part * LANES, (part + 1) * LANES)
            copy(flat.at[plane, part], fields_ref.at[plane // 2, 0, plane % 2, :, lanes])
    finish()


def depth_steps(pieces, before, after, src, rec, sizes):
    row_count, steps, halo, vel_halo = sizes
    width = pieces[0].shape[-1]
    owners = len(pieces)
    rows = row_count + 2 * halo
    parts = owners * width // LANES
    tall = row_count + 2 * vel_halo
    there = pl.BlockSpec(memory_space=pltpu.HBM)
    return pl.pallas_call(
        functools.partial(depth_kernel, sizes),
        out_shape=(
            jax.ShapeDtypeStruct((2, 1, 2, row_count, owners * width), jnp.float32),
            *[jax.ShapeDtypeStruct((steps, row_count, width), jnp.float32)] * owners,
        ),
        in_specs=[there] * (owners + 4),
        out_specs=(there,) * (owners + 1),
        scratch_shapes=[
            pltpu.VMEM((PASSES + 1, 4, parts, rows + 2 * SUB, LANES), jnp.float32),
            pltpu.VMEM((4, parts, rows + 2 * SUB, LANES), jnp.float32),
            pltpu.VMEM((steps, parts, tall + 2 * SUB, LANES), jnp.float32),
            pltpu.VMEM((4 + steps, parts, row_count, LANES), jnp.float32),
            pltpu.SemaphoreType.DMA((4 + 3 * parts + (4 + steps) * parts,)),
        ],
        cost_estimate=pl.CostEstimate(
            flops=steps * 300 * rows * owners * width, bytes_accessed=64 * rows * owners * width, transcendentals=0
        ),
        name="depth",
    )(*pieces, before, after, src, rec)


def shifts(axis):
    count = lax.axis_size(axis)
    return [[(i, (i + k) % count) for i in range(count)] for k in range(1, count)]


def body(velocity, src_cell, src_wave, rec_cell, rec_data):
    steps, row_count, width = velocity.shape
    freqs, tiles = lax.axis_size("freq"), lax.axis_size("tile")
    assert width % LANES == 0 and width * freqs % (2 * LANES) == 0 and row_count % SUB == 0
    me = lax.axis_index("freq")
    halo = PASSES * steps
    vel_halo = round_up(PASSES * (steps - 1), SUB)
    rows = row_count + 2 * halo
    sizes = (row_count, steps, halo, vel_halo)

    cols = width * freqs
    others = [lax.ppermute(velocity, "freq", pairs) for pairs in shifts("freq")]
    src = inject(src_cell, src_wave, rows, halo, row_count, cols)
    others, src = lax.optimization_barrier((others, src))
    pieces = [velocity] + others
    up = [(i, i + 1) for i in range(tiles - 1)]
    down = [(j, i) for i, j in up]
    lowest = jnp.stack([p[:, row_count - vel_halo :] for p in pieces])
    highest = jnp.stack([p[:, :vel_halo] for p in pieces])
    lowest, highest, rec_cell = lax.optimization_barrier((lowest, highest, rec_cell))
    before = lax.ppermute(lowest, "tile", up)
    after = lax.ppermute(highest, "tile", down)
    rec = inject(rec_cell, rec_data, rows, halo, row_count, cols)
    fields, total, *images = depth_steps(pieces, before, after, src, rec, sizes)
    for image, pairs in zip(images, shifts("freq")):
        total = total + lax.ppermute(image, "freq", pairs)
    return fields, total


def solution(mesh):
    placed = (
        P(None, "tile", "freq"),
        P("shots"),
        P(None, "freq", "shots"),
        P("shots"),
        P(None, "freq", "shots"),
    )
    return jax.shard_map(
        body,
        mesh=mesh,
        in_specs=placed,
        out_specs=(P("shots", "freq", None, "tile", None), P("shots", "tile", "freq")),
        check_vma=False,
    )
```

```python
import functools

import jax
import jax.numpy as jnp
from jax import lax
from jax.experimental import pallas as pl
from jax.experimental.pallas import tpu as pltpu
from jax.sharding import PartitionSpec as P

PASSES = 5
LANES = 128
SUB = 8
CHUNK = 1024
UNROLL = 4
BLOCK = 256

term_weights = (0.3, 0.25, -0.15, 0.12, -0.1, 0.08)
phase_unit = 0.25
slowest = 1.5


def round_up(value, unit):
    return -(-value // unit) * unit


def inject_kernel(rows, halo, row_count, cell_ref, wave_ref, out_ref):
    chunk = min(CHUNK, cell_ref.shape[0] * LANES)
    chunks = cell_ref.shape[0] * LANES // chunk
    blocks = out_ref.shape[1] // 2
    pair = 2 * LANES
    cols = blocks * pair
    high_count = blocks * rows
    tall = 2 * SUB
    first = lax.axis_index("tile") * row_count - halo
    size = min(BLOCK, max(high_count, pair))
    ids = lax.broadcasted_iota(jnp.int32, (size, LANES), 0).astype(jnp.float32).astype(jnp.bfloat16)

    def spread(values, line, count):
        one = jnp.broadcast_to(values[line : line + 1], (tall, LANES)).astype(jnp.bfloat16)
        return jnp.concatenate([one] * (count // tall), axis=0)

    def one_hot(index, line, count):
        return jnp.maximum(1.0 - jnp.abs(ids[:count] - spread(index, line, count)), 0.0)

    def add(index):
        lines = chunk // LANES
        lefts, rights = [], []
        for group in range(0, lines, SUB):
            height = min(SUB, lines)
            at = pl.ds(pl.multiple_of(index * lines + group, height), height)
            cell = cell_ref[at, :]
            row = cell // cols - first
            col = cell % cols
            high = jnp.where((row >= 0) & (row < rows), col // pair * rows + row, -1)
            low = ((col % 2) * LANES + col % pair // 2).astype(jnp.float32)
            pieces = []
            for part in range(2):
                value = wave_ref[part, at, :]
                top = value.astype(jnp.bfloat16).astype(jnp.float32)
                pieces += [top, value - top]
            for line in range(height):
                rights.append(one_hot(low, line, pair))
                variants = [[] for _ in pieces]
                for base in range(0, high_count, size):
                    count = min(size, high_count - base)
                    match = one_hot((high - base).astype(jnp.float32), line, count)
                    for variant, piece in zip(variants, pieces):
                        variant.append(match * spread(piece, line, count))
                lefts.append(jnp.concatenate(sum(variants, []), axis=0))
        total = lax.dot_general(
            jnp.concatenate(lefts, axis=1),
            jnp.concatenate(rights, axis=1),
            (((1,), (1,)), ((), ())),
            preferred_element_type=jnp.float32,
        )
        for part in range(2):
            at = 2 * part * high_count
            both = total[at : at + high_count] + total[at + high_count : at + 2 * high_count]
            for odd in range(2):
                out_at = slice(odd * blocks, (odd + 1) * blocks)
                out_ref[part, out_at] = out_ref[part, out_at] + both[:, odd * LANES : (odd + 1) * LANES].reshape(
                    blocks, rows, LANES
                )

    out_ref[...] = jnp.zeros_like(out_ref)
    unroll = next(u for u in (UNROLL, 2, 1) if chunks % u == 0)

    def some_chunks(index, carry):
        for one in range(unroll):
            add(index * unroll + one)
        return carry

    lax.fori_loop(0, chunks // unroll, some_chunks, 0)


def inject(cells, waves, rows, halo, row_count, cols):
    points = cells.shape[0]
    whole = pl.BlockSpec(memory_space=pltpu.VMEM)
    return pl.pallas_call(
        functools.partial(inject_kernel, rows, halo, row_count),
        out_shape=pltpu.VMEM((2, cols // LANES, rows, LANES), jnp.float32),
        in_specs=[whole, whole],
        out_specs=whole,
        cost_estimate=pl.CostEstimate(
            flops=8 * rows * cols * points, bytes_accessed=12 * points, transcendentals=0
        ),
        name="inject",
    )(cells.reshape(points // LANES, LANES), waves.reshape(2, points // LANES, LANES))


def sine(angle, square, terms):
    total = None
    for k in range(terms - 1, 0, -1):
        coef = 1.0
        for m in range(2, 2 * k + 2):
            coef /= m
        coef = coef if k % 2 == 0 else -coef
        total = coef if total is None else total * square + coef
    return angle * (total * square + 1.0)


def cosine(square, terms):
    total = None
    for k in range(terms - 1, 0, -1):
        coef = 1.0
        for m in range(2, 2 * k + 1):
            coef /= m
        coef = coef if k % 2 == 0 else -coef
        total = coef if total is None else total * square + coef
    return total * square + 1.0


def terms_for(largest, offset):
    count, size = 1, largest * largest / ((1 + offset) * (2 + offset))
    while size > 3e-8 or count < 2:
        count += 1
        size *= largest * largest / ((2 * count - 1 + offset) * (2 * count + offset))
    return count


def times(a, b):
    return a[0] * b[0] - a[1] * b[1], a[0] * b[1] + a[1] * b[0]


def squared(a):
    twice = a[1] + a[1]
    return 1.0 - twice * a[1], twice * a[0]


def coefficients(speed, number, limit):
    slow = (0.2 * phase_unit) * number / jnp.maximum(speed, 1.0)
    square = slow * slow
    sines, cosines = terms_for(0.2 * limit, 1), terms_for(0.2 * limit, 0)
    a20 = (cosine(square, cosines), sine(slow, square, sines))
    small, square = slow * 0.75, square * 0.5625
    a15 = (cosine(square, cosines), sine(small, square, sines))
    a30 = squared(a15)
    a45 = times(a30, a15)
    a60 = squared(a30)
    a80 = times(a60, a20)
    a100 = times(a80, a20)
    angles = (a100, a80, a60, a45, a30, a20)
    return [(weight * a[0], weight * a[1]) for weight, a in zip(term_weights, angles)]


def depth_kernel(sizes, *refs):
    row_count, steps, halo, vel_halo = sizes
    freqs = lax.axis_size("freq")
    tiles = lax.axis_size("tile")
    pieces, (before_ref, after_ref, src_ref, rec_ref) = refs[:freqs], refs[freqs : freqs + 4]
    fields_ref, *image_refs, terms, sums, speed, flat, sem = refs[freqs + 4 :]
    me = lax.axis_index("freq")
    tile = lax.axis_index("tile")
    number = (me + 1).astype(jnp.float32)
    limit = freqs * phase_unit / slowest
    rows = row_count + 2 * halo
    parts = src_ref.shape[1]
    blocks = parts // 2
    width = pieces[0].shape[-1]
    per_owner = width // LANES

    pending = []

    def copy(src, dst):
        pending.append(pltpu.make_async_copy(src, dst, sem.at[copy.started]))
        pending[-1].start()
        copy.started += 1

    def finish():
        while pending:
            pending.pop(0).wait()

    copy.started = 0
    for back, piece in enumerate(pieces):
        owner = lax.rem(me + freqs - back, freqs)
        for part in range(per_owner):
            lanes = slice(part * LANES, (part + 1) * LANES)
            for ref, low, size in (
                (piece, vel_halo, row_count),
                (before_ref.at[back], 0, vel_halo),
                (after_ref.at[back], vel_halo + row_count, vel_halo),
            ):
                copy(ref.at[:, :, lanes], speed.at[:, owner * per_owner + part, low : low + size, :])

    shape = (SUB, LANES)
    lane = lax.broadcasted_iota(jnp.int32, shape, 1)
    sub = lax.broadcasted_iota(jnp.int32, shape, 0)
    first_lane, last_lane = lane == 0, lane == LANES - 1
    zero = jnp.zeros(shape, jnp.float32)
    edges = (
        (halo - 1, jnp.where(tile == 0, 0.0, 1.0)),
        (halo + row_count, jnp.where(tile == tiles - 1, 0.0, 1.0)),
    )

    def strided(low, count, index=0):
        return pl.ds(low + index, SUB, stride=count)

    def take(value, index):
        return jnp.take_along_axis(value, index, axis=1, mode="promise_in_bounds")

    def split(low, high):
        index = (2 * lane) % LANES
        return [
            jnp.where(lane < LANES // 2, take(low, index + odd), take(high, index + odd)) for odd in range(2)
        ]

    def join(even, odd):
        index = lane // 2
        return [
            jnp.where(lane % 2 == 1, take(odd, index + at), take(even, index + at)) for at in (0, LANES // 2)
        ]

    def share(low, high):
        count = -(-(high - low) // SUB)
        return count + (count % SUB == 0)

    def one_pass(plane, order, low, high):
        count = share(low, high)
        keeps = {}
        for row, keep in edges:
            at, index = divmod(row - low, count)
            if 0 <= at < SUB:
                keeps.setdefault(index, []).append(jnp.where(sub == at, keep, 1.0))

        def load(part, index):
            return terms[order - 1, plane, part, strided(low, count, index), :]

        here = [load(part, 0) for part in range(parts)]
        pair = [load(part, -1) + here[part] for part in range(parts)]
        for index in range(count):
            below = [load(part, index + 1) for part in range(parts)]
            next_pair = [here[part] + below[part] for part in range(parts)]
            stacked = [pair[part] + next_pair[part] for part in range(parts)]
            moved = [pltpu.roll(v, LANES - 1 if part < blocks else 1, 1) for part, v in enumerate(stacked)]
            for part in range(parts):
                blk = part % blocks
                even, odd = stacked[blk], stacked[blocks + blk]
                if part < blocks:
                    other = moved[part + blocks - 1] if blk > 0 else zero
                    side = jnp.where(first_lane, other, moved[part + blocks])
                    total = (even + odd) + even + side
                else:
                    other = moved[blk + 1] if blk + 1 < blocks else zero
                    side = jnp.where(last_lane, other, moved[blk])
                    total = (even + odd) + odd + side
                at = strided(low, count, index)
                if order == 1:
                    total = 0.125 * total
                else:
                    total = 0.25 * total - sums[plane, part, at, :]
                new = total - here[part]
                for keep in keeps.get(index, []):
                    new = new * keep
                    total = total * keep
                if order < PASSES:
                    sums[plane, part, at, :] = total
                terms[order, plane, part, at, :] = new
            here, pair = below, next_pair

    for field, ref in enumerate((src_ref, rec_ref)):
        for part in range(2):
            terms[0, 2 * field + part, :, :rows, :] = ref[part]

    def put(slot, blk, at, pair):
        for half, value in enumerate(join(*pair)):
            flat[slot, 2 * blk + half, at, :] = value

    for step in range(steps):

        def passes(plane, carry):
            for order in range(1, PASSES + 1):
                one_pass(plane, order, PASSES * step + order, rows - PASSES * step - order)
            return carry

        lax.fori_loop(0, 4, passes, 0)
        low, high = PASSES * (step + 1), rows - PASSES * (step + 1)
        count = share(low, high)
        last = step == steps - 1
        if step == 0:
            finish()

        def blend(index, carry):
            at = strided(low, count, index)
            vel_at = strided(low - halo + vel_halo, count, index)
            for blk in range(blocks):
                done = []
                speeds = split(*[speed[step, 2 * blk + half, vel_at, :] for half in range(2)])
                for odd in range(2):
                    part = odd * blocks + blk
                    coefs = coefficients(speeds[odd], number, limit)
                    results = []
                    for field in range(2):
                        real, imag = [], []
                        for order, (cr, ci) in enumerate(coefs):
                            tr = terms[order, 2 * field, part, at, :]
                            ti = terms[order, 2 * field + 1, part, at, :]
                            if field == 0:
                                real += [cr * tr - ci * ti]
                                imag += [cr * ti + ci * tr]
                            else:
                                real += [cr * tr + ci * ti]
                                imag += [cr * ti - ci * tr]
                        results += [sum(real[1:], real[0]), sum(imag[1:], imag[0])]
                    if last:
                        results.append(results[0] * results[2] + results[1] * results[3])
                    else:
                        for plane in range(4):
                            terms[0, plane, part, at, :] = results[plane]
                    done.append(results)
                if last:
                    out_at = strided(0, count, index)
                    for slot, pair in zip((0, 1, 2, 3, 4 + step), zip(*done)):
                        put(slot, blk, out_at, pair)
            return carry

        lax.fori_loop(0, count, blend, 0)
        if not last:
            image_count = row_count // SUB

            def correlate(index, carry):
                for blk in range(blocks):
                    pair = []
                    for odd in range(2):
                        field = [
                            terms[0, plane, odd * blocks + blk, strided(halo, image_count, index), :]
                            for plane in range(4)
                        ]
                        pair.append(field[0] * field[2] + field[1] * field[3])
                    put(4 + step, blk, strided(0, image_count, index), pair)
                return carry

            lax.fori_loop(0, image_count, correlate, 0)

        for other, ref in enumerate(image_refs):
            cores, places = len(image_refs), ref.shape[0]
            core, place = lax.rem(me, cores), lax.div(me, cores)
            for ahead in range(places):
                owner = lax.rem(place + ahead, places) * cores + lax.rem(core + other, cores)
                for part in range(per_owner):
                    lanes = slice(part * LANES, (part + 1) * LANES)
                    ref[ahead, step, :, lanes] = flat[4 + step, owner * per_owner + part]
    for plane in range(4):
        for part in range(parts):
            lanes = slice(part * LANES, (part + 1) * LANES)
            fields_ref[plane // 2, 0, plane % 2, :, lanes] = flat[plane, part]


def depth_steps(pieces, before, after, src, rec, sizes):
    row_count, steps, halo, vel_halo = sizes
    width = pieces[0].shape[-1]
    owners = len(pieces)
    rows = row_count + 2 * halo
    parts = owners * width // LANES
    tall = row_count + 2 * vel_halo
    whole = pl.BlockSpec(memory_space=pltpu.VMEM)
    cores = cores_of(owners)
    return pl.pallas_call(
        functools.partial(depth_kernel, sizes),
        out_shape=(
            pltpu.VMEM((2, 1, 2, row_count, owners * width), jnp.float32),
            *[pltpu.VMEM((owners // cores, steps, row_count, width), jnp.float32)] * cores,
        ),
        in_specs=[whole] * (owners + 4),
        out_specs=(whole,) * (cores + 1),
        scratch_shapes=[
            pltpu.VMEM((PASSES + 1, 4, parts, rows + 2 * SUB, LANES), jnp.float32),
            pltpu.VMEM((4, parts, rows + 2 * SUB, LANES), jnp.float32),
            pltpu.VMEM((steps, parts, tall + 2 * SUB, LANES), jnp.float32),
            pltpu.VMEM((4 + steps, parts, row_count, LANES), jnp.float32),
            pltpu.SemaphoreType.DMA((3 * parts,)),
        ],
        cost_estimate=pl.CostEstimate(
            flops=steps * 300 * rows * owners * width, bytes_accessed=64 * rows * owners * width, transcendentals=0
        ),
        name="depth",
    )(*[pltpu.with_memory_space_constraint(one, pltpu.VMEM) for one in (*pieces, before, after, src, rec)])


def cores_of(freqs):
    return 2 - freqs % 2


def shifts(axis):
    count = lax.axis_size(axis)
    return [[(i, (i + k) % count) for i in range(count)] for k in range(1, count)]


def body(velocity, src_cell, src_wave, rec_cell, rec_data):
    steps, row_count, width = velocity.shape
    freqs, tiles = lax.axis_size("freq"), lax.axis_size("tile")
    assert width % LANES == 0 and width * freqs % (2 * LANES) == 0 and row_count % SUB == 0
    me = lax.axis_index("freq")
    halo = PASSES * steps
    vel_halo = round_up(PASSES * (steps - 1), SUB)
    rows = row_count + 2 * halo
    sizes = (row_count, steps, halo, vel_halo)

    cols = width * freqs
    others = [lax.ppermute(velocity, "freq", pairs) for pairs in shifts("freq")]
    src = inject(src_cell, src_wave, rows, halo, row_count, cols)
    others, src = lax.optimization_barrier((others, src))
    pieces = [velocity] + others
    up = [(i, i + 1) for i in range(tiles - 1)]
    down = [(j, i) for i, j in up]
    lowest = jnp.stack([p[:, row_count - vel_halo :] for p in pieces])
    highest = jnp.stack([p[:, :vel_halo] for p in pieces])
    lowest, highest, rec_cell = lax.optimization_barrier((lowest, highest, rec_cell))
    before = lax.ppermute(lowest, "tile", up)
    after = lax.ppermute(highest, "tile", down)
    rec = inject(rec_cell, rec_data, rows, halo, row_count, cols)
    fields, *images = depth_steps(pieces, before, after, src, rec, sizes)
    cores = cores_of(freqs)
    sums = images[0]
    for other in range(1, cores):
        swap = [(i, i - i % cores + (i + other) % cores) for i in range(freqs)]
        sums = sums + lax.ppermute(images[other], "freq", swap)
    total = sums[0]
    for ahead in range(1, freqs // cores):
        along = [(i, (i + ahead * cores) % freqs) for i in range(freqs)]
        total = total + lax.ppermute(sums[ahead], "freq", along)
    return fields, total


def solution(mesh):
    placed = (
        P(None, "tile", "freq"),
        P("shots"),
        P(None, "freq", "shots"),
        P("shots"),
        P(None, "freq", "shots"),
    )
    return jax.shard_map(
        body,
        mesh=mesh,
        in_specs=placed,
        out_specs=(P("shots", "freq", None, "tile", None), P("shots", "tile", "freq")),
        check_vma=False,
    )
```

```python
import functools

import jax
import jax.numpy as jnp
from jax import lax
from jax.experimental import pallas as pl
from jax.experimental.pallas import tpu as pltpu
from jax.sharding import PartitionSpec as P

PASSES = 5
LANES = 128
SUB = 8
CHUNK = 1024
UNROLL = 4
EARLY = 4
BLOCK = 256

term_weights = (0.3, 0.25, -0.15, 0.12, -0.1, 0.08)
phase_unit = 0.25
slowest = 1.5


def round_up(value, unit):
    return -(-value // unit) * unit


def inject_kernel(rows, halo, row_count, spans, *refs):
    points = [refs[2 * job : 2 * job + 2] for job in range(len(spans))]
    extra_ref, *outs = refs[2 * len(spans) :]
    blocks = outs[0].shape[1] // 2
    pair = 2 * LANES
    cols = blocks * pair
    high_count = blocks * rows
    tall = 2 * SUB
    first = lax.axis_index("tile") * row_count - halo
    size = min(BLOCK, max(high_count, pair))
    ids = lax.broadcasted_iota(jnp.int32, (size, LANES), 0).astype(jnp.float32).astype(jnp.bfloat16)

    def spread(values, line, count):
        one = jnp.broadcast_to(values[line : line + 1], (tall, LANES)).astype(jnp.bfloat16)
        return jnp.concatenate([one] * (count // tall), axis=0)

    def one_hot(index, line, count):
        return jnp.maximum(1.0 - jnp.abs(ids[:count] - spread(index, line, count)), 0.0)

    def add(cell_ref, wave_ref, out_ref, index):
        lines = CHUNK // LANES
        lefts, rights = [], []
        for group in range(0, lines, SUB):
            height = min(SUB, lines)
            at = pl.ds(pl.multiple_of(index * lines + group, height), height)
            cell = cell_ref[at, :]
            row = cell // cols - first
            col = cell % cols
            high = jnp.where((row >= 0) & (row < rows), col // pair * rows + row, -1)
            low = ((col % 2) * LANES + col % pair // 2).astype(jnp.float32)
            pieces = []
            for part in range(2):
                value = wave_ref[part, at, :]
                top = value.astype(jnp.bfloat16).astype(jnp.float32)
                pieces += [top, value - top]
            for line in range(height):
                rights.append(one_hot(low, line, pair))
                variants = [[] for _ in pieces]
                for base in range(0, high_count, size):
                    count = min(size, high_count - base)
                    match = one_hot((high - base).astype(jnp.float32), line, count)
                    for variant, piece in zip(variants, pieces):
                        variant.append(match * spread(piece, line, count))
                lefts.append(jnp.concatenate(sum(variants, []), axis=0))
        total = lax.dot_general(
            jnp.concatenate(lefts, axis=1),
            jnp.concatenate(rights, axis=1),
            (((1,), (1,)), ((), ())),
            preferred_element_type=jnp.float32,
        )
        for part in range(2):
            at = 2 * part * high_count
            both = total[at : at + high_count] + total[at + high_count : at + 2 * high_count]
            for odd in range(2):
                out_at = slice(odd * blocks, (odd + 1) * blocks)
                out_ref[part, out_at] = out_ref[part, out_at] + both[:, odd * LANES : (odd + 1) * LANES].reshape(
                    blocks, rows, LANES
                )

    def run(job, out_ref):
        begin, end = spans[job]
        unroll = next(u for u in (UNROLL, 2, 1) if (end - begin) % u == 0)

        def some_chunks(index, carry):
            for one in range(unroll):
                add(*points[job], out_ref, begin + index * unroll + one)
            return carry

        lax.fori_loop(0, (end - begin) // unroll, some_chunks, 0)

    if len(spans) == 1:
        outs[0][...] = extra_ref[...]
        run(0, outs[0])
        return
    *outs, moved_ref, sem = outs
    move = pltpu.make_async_copy(extra_ref, moved_ref, sem)
    move.start()
    for job, out_ref in enumerate(outs):
        out_ref[...] = jnp.zeros_like(out_ref)
        run(job, out_ref)
    move.wait()


def inject(jobs, extra, rows, halo, row_count, cols):
    whole = pl.BlockSpec(memory_space=pltpu.VMEM)
    alone = len(jobs) == 1
    operands = []
    for cells, waves, _, _ in jobs:
        lines = cells.shape[0] // LANES
        operands += [cells.reshape(lines, LANES), waves.reshape(2, lines, LANES)]
    total = sum(end - begin for *_, begin, end in jobs) * CHUNK
    planes = pltpu.VMEM((2, cols // LANES, rows, LANES), jnp.float32)
    outs = [planes] * len(jobs) + ([] if alone else [pltpu.VMEM(extra.shape, extra.dtype)])
    return pl.pallas_call(
        functools.partial(inject_kernel, rows, halo, row_count, [job[2:] for job in jobs]),
        out_shape=outs,
        in_specs=[whole] * len(operands) + [whole if alone else pl.BlockSpec(memory_space=pltpu.HBM)],
        out_specs=[whole] * len(outs),
        scratch_shapes=[] if alone else [pltpu.SemaphoreType.DMA(())],
        cost_estimate=pl.CostEstimate(
            flops=8 * rows * cols * total, bytes_accessed=12 * total, transcendentals=0
        ),
        name="inject",
    )(*operands, pltpu.with_memory_space_constraint(extra, pltpu.VMEM) if alone else extra)


def sine(angle, square, terms):
    total = None
    for k in range(terms - 1, 0, -1):
        coef = 1.0
        for m in range(2, 2 * k + 2):
            coef /= m
        coef = coef if k % 2 == 0 else -coef
        total = coef if total is None else total * square + coef
    return angle * (total * square + 1.0)


def cosine(square, terms):
    total = None
    for k in range(terms - 1, 0, -1):
        coef = 1.0
        for m in range(2, 2 * k + 1):
            coef /= m
        coef = coef if k % 2 == 0 else -coef
        total = coef if total is None else total * square + coef
    return total * square + 1.0


def terms_for(largest, offset):
    count, size = 1, largest * largest / ((1 + offset) * (2 + offset))
    while size > 3e-8 or count < 2:
        count += 1
        size *= largest * largest / ((2 * count - 1 + offset) * (2 * count + offset))
    return count


def times(a, b):
    return a[0] * b[0] - a[1] * b[1], a[0] * b[1] + a[1] * b[0]


def squared(a):
    twice = a[1] + a[1]
    return 1.0 - twice * a[1], twice * a[0]


def coefficients(speed, number, limit):
    slow = (0.2 * phase_unit) * number / jnp.maximum(speed, 1.0)
    square = slow * slow
    sines, cosines = terms_for(0.2 * limit, 1), terms_for(0.2 * limit, 0)
    a20 = (cosine(square, cosines), sine(slow, square, sines))
    small, square = slow * 0.75, square * 0.5625
    a15 = (cosine(square, cosines), sine(small, square, sines))
    a30 = squared(a15)
    a45 = times(a30, a15)
    a60 = squared(a30)
    a80 = times(a60, a20)
    a100 = times(a80, a20)
    angles = (a100, a80, a60, a45, a30, a20)
    return [(weight * a[0], weight * a[1]) for weight, a in zip(term_weights, angles)]


def depth_kernel(sizes, *refs):
    row_count, steps, halo, vel_halo = sizes
    freqs = lax.axis_size("freq")
    tiles = lax.axis_size("tile")
    pieces, (before_ref, after_ref, src_ref, rec_ref) = refs[:freqs], refs[freqs : freqs + 4]
    fields_ref, *image_refs, terms, sums, speed, flat, sem = refs[freqs + 4 :]
    me = lax.axis_index("freq")
    tile = lax.axis_index("tile")
    number = (me + 1).astype(jnp.float32)
    limit = freqs * phase_unit / slowest
    rows = row_count + 2 * halo
    parts = src_ref.shape[1]
    blocks = parts // 2
    width = pieces[0].shape[-1]
    per_owner = width // LANES

    pending = []

    def copy(src, dst):
        pending.append(pltpu.make_async_copy(src, dst, sem.at[copy.started]))
        pending[-1].start()
        copy.started += 1

    def finish():
        while pending:
            pending.pop(0).wait()

    copy.started = 0
    for back, piece in enumerate(pieces):
        owner = lax.rem(me + freqs - back, freqs)
        for part in range(per_owner):
            lanes = slice(part * LANES, (part + 1) * LANES)
            for ref, low, size in (
                (piece, vel_halo, row_count),
                (before_ref.at[back], 0, vel_halo),
                (after_ref.at[back], vel_halo + row_count, vel_halo),
            ):
                copy(ref.at[:, :, lanes], speed.at[:, owner * per_owner + part, low : low + size, :])

    shape = (SUB, LANES)
    lane = lax.broadcasted_iota(jnp.int32, shape, 1)
    sub = lax.broadcasted_iota(jnp.int32, shape, 0)
    first_lane, last_lane = lane == 0, lane == LANES - 1
    zero = jnp.zeros(shape, jnp.float32)
    edges = (
        (halo - 1, jnp.where(tile == 0, 0.0, 1.0)),
        (halo + row_count, jnp.where(tile == tiles - 1, 0.0, 1.0)),
    )

    def strided(low, count, index=0):
        return pl.ds(low + index, SUB, stride=count)

    def take(value, index):
        return jnp.take_along_axis(value, index, axis=1, mode="promise_in_bounds")

    def split(low, high):
        index = (2 * lane) % LANES
        return [
            jnp.where(lane < LANES // 2, take(low, index + odd), take(high, index + odd)) for odd in range(2)
        ]

    def join(even, odd):
        index = lane // 2
        return [
            jnp.where(lane % 2 == 1, take(odd, index + at), take(even, index + at)) for at in (0, LANES // 2)
        ]

    def share(low, high):
        count = -(-(high - low) // SUB)
        return count + (count % SUB == 0)

    def one_pass(plane, order, low, high):
        count = share(low, high)
        keeps = {}
        for row, keep in edges:
            at, index = divmod(row - low, count)
            if 0 <= at < SUB:
                keeps.setdefault(index, []).append(jnp.where(sub == at, keep, 1.0))

        def load(part, index):
            return terms[order - 1, plane, part, strided(low, count, index), :]

        here = [load(part, 0) for part in range(parts)]
        pair = [load(part, -1) + here[part] for part in range(parts)]
        for index in range(count):
            below = [load(part, index + 1) for part in range(parts)]
            next_pair = [here[part] + below[part] for part in range(parts)]
            stacked = [pair[part] + next_pair[part] for part in range(parts)]
            moved = [pltpu.roll(v, LANES - 1 if part < blocks else 1, 1) for part, v in enumerate(stacked)]
            for part in range(parts):
                blk = part % blocks
                even, odd = stacked[blk], stacked[blocks + blk]
                if part < blocks:
                    other = moved[part + blocks - 1] if blk > 0 else zero
                    side = jnp.where(first_lane, other, moved[part + blocks])
                    total = (even + odd) + even + side
                else:
                    other = moved[blk + 1] if blk + 1 < blocks else zero
                    side = jnp.where(last_lane, other, moved[blk])
                    total = (even + odd) + odd + side
                at = strided(low, count, index)
                if order == 1:
                    total = 0.125 * total
                else:
                    total = 0.25 * total - sums[plane, part, at, :]
                new = total - here[part]
                for keep in keeps.get(index, []):
                    new = new * keep
                    total = total * keep
                if order < PASSES:
                    sums[plane, part, at, :] = total
                terms[order, plane, part, at, :] = new
            here, pair = below, next_pair

    for field, ref in enumerate((src_ref, rec_ref)):
        for part in range(2):
            terms[0, 2 * field + part, :, :rows, :] = ref[part]

    def put(slot, blk, at, pair):
        for half, value in enumerate(join(*pair)):
            flat[slot, 2 * blk + half, at, :] = value

    for step in range(steps):

        def passes(plane, carry):
            for order in range(1, PASSES + 1):
                one_pass(plane, order, PASSES * step + order, rows - PASSES * step - order)
            return carry

        lax.fori_loop(0, 4, passes, 0)
        low, high = PASSES * (step + 1), rows - PASSES * (step + 1)
        count = share(low, high)
        last = step == steps - 1
        if step == 0:
            finish()

        def blend(index, carry):
            at = strided(low, count, index)
            vel_at = strided(low - halo + vel_halo, count, index)
            for blk in range(blocks):
                done = []
                speeds = split(*[speed[step, 2 * blk + half, vel_at, :] for half in range(2)])
                for odd in range(2):
                    part = odd * blocks + blk
                    coefs = coefficients(speeds[odd], number, limit)
                    results = []
                    for field in range(2):
                        real, imag = [], []
                        for order, (cr, ci) in enumerate(coefs):
                            tr = terms[order, 2 * field, part, at, :]
                            ti = terms[order, 2 * field + 1, part, at, :]
                            if field == 0:
                                real += [cr * tr - ci * ti]
                                imag += [cr * ti + ci * tr]
                            else:
                                real += [cr * tr + ci * ti]
                                imag += [cr * ti - ci * tr]
                        results += [sum(real[1:], real[0]), sum(imag[1:], imag[0])]
                    if last:
                        results.append(results[0] * results[2] + results[1] * results[3])
                    else:
                        for plane in range(4):
                            terms[0, plane, part, at, :] = results[plane]
                    done.append(results)
                if last:
                    out_at = strided(0, count, index)
                    for slot, pair in zip((0, 1, 2, 3, 4 + step), zip(*done)):
                        put(slot, blk, out_at, pair)
            return carry

        lax.fori_loop(0, count, blend, 0)
        if not last:
            image_count = row_count // SUB

            def correlate(index, carry):
                for blk in range(blocks):
                    pair = []
                    for odd in range(2):
                        field = [
                            terms[0, plane, odd * blocks + blk, strided(halo, image_count, index), :]
                            for plane in range(4)
                        ]
                        pair.append(field[0] * field[2] + field[1] * field[3])
                    put(4 + step, blk, strided(0, image_count, index), pair)
                return carry

            lax.fori_loop(0, image_count, correlate, 0)

        for other, ref in enumerate(image_refs):
            cores, places = len(image_refs), ref.shape[0]
            core, place = lax.rem(me, cores), lax.div(me, cores)
            for ahead in range(places):
                owner = lax.rem(place + ahead, places) * cores + lax.rem(core + other, cores)
                for part in range(per_owner):
                    lanes = slice(part * LANES, (part + 1) * LANES)
                    ref[ahead, step, :, lanes] = flat[4 + step, owner * per_owner + part]
    for plane in range(4):
        for part in range(parts):
            lanes = slice(part * LANES, (part + 1) * LANES)
            fields_ref[plane // 2, 0, plane % 2, :, lanes] = flat[plane, part]


def depth_steps(pieces, before, after, src, rec, sizes):
    row_count, steps, halo, vel_halo = sizes
    width = pieces[0].shape[-1]
    owners = len(pieces)
    rows = row_count + 2 * halo
    parts = owners * width // LANES
    tall = row_count + 2 * vel_halo
    whole = pl.BlockSpec(memory_space=pltpu.VMEM)
    cores = cores_of(owners)
    return pl.pallas_call(
        functools.partial(depth_kernel, sizes),
        out_shape=(
            pltpu.VMEM((2, 1, 2, row_count, owners * width), jnp.float32),
            *[pltpu.VMEM((owners // cores, steps, row_count, width), jnp.float32)] * cores,
        ),
        in_specs=[whole] * (owners + 4),
        out_specs=(whole,) * (cores + 1),
        scratch_shapes=[
            pltpu.VMEM((PASSES + 1, 4, parts, rows + 2 * SUB, LANES), jnp.float32),
            pltpu.VMEM((4, parts, rows + 2 * SUB, LANES), jnp.float32),
            pltpu.VMEM((steps, parts, tall + 2 * SUB, LANES), jnp.float32),
            pltpu.VMEM((4 + steps, parts, row_count, LANES), jnp.float32),
            pltpu.SemaphoreType.DMA((3 * parts,)),
        ],
        cost_estimate=pl.CostEstimate(
            flops=steps * 300 * rows * owners * width, bytes_accessed=64 * rows * owners * width, transcendentals=0
        ),
        name="depth",
        compiler_params=pltpu.CompilerParams(),
    )(*[pltpu.with_memory_space_constraint(one, pltpu.VMEM) for one in (*pieces, before, after, src, rec)])


def cores_of(freqs):
    return 2 - freqs % 2


def shifts(axis):
    count = lax.axis_size(axis)
    return [[(i, (i + k) % count) for i in range(count)] for k in range(1, count)]


def body(velocity, src_cell, src_wave, rec_cell, rec_data):
    steps, row_count, width = velocity.shape
    freqs, tiles = lax.axis_size("freq"), lax.axis_size("tile")
    assert src_cell.shape[0] % CHUNK == 0 and rec_cell.shape[0] % (EARLY * CHUNK) == 0
    assert width % LANES == 0 and width * freqs % (2 * LANES) == 0 and row_count % SUB == 0
    me = lax.axis_index("freq")
    halo = PASSES * steps
    vel_halo = round_up(PASSES * (steps - 1), SUB)
    rows = row_count + 2 * halo
    sizes = (row_count, steps, halo, vel_halo)

    cols = width * freqs
    others = [lax.ppermute(velocity, "freq", pairs) for pairs in shifts("freq")]
    src_chunks, rec_chunks = src_cell.shape[0] // CHUNK, rec_cell.shape[0] // CHUNK
    early = rec_chunks // EARLY
    jobs = [(src_cell, src_wave, 0, src_chunks), (rec_cell, rec_data, 0, early)]
    src, rec, own = inject(jobs, velocity, rows, halo, row_count, cols)
    others, src, own = lax.optimization_barrier((others, src, own))
    pieces = [own] + others
    up = [(i, i + 1) for i in range(tiles - 1)]
    down = [(j, i) for i, j in up]
    lowest = jnp.stack([p[:, row_count - vel_halo :] for p in pieces])
    highest = jnp.stack([p[:, :vel_halo] for p in pieces])
    lowest, highest, rec = lax.optimization_barrier((lowest, highest, rec))
    before = lax.ppermute(lowest, "tile", up)
    after = lax.ppermute(highest, "tile", down)
    (rec,) = inject([(rec_cell, rec_data, early, rec_chunks)], rec, rows, halo, row_count, cols)
    fields, *images = depth_steps(pieces, before, after, src, rec, sizes)
    cores = cores_of(freqs)
    sums = images[0]
    for other in range(1, cores):
        swap = [(i, i - i % cores + (i + other) % cores) for i in range(freqs)]
        sums = sums + lax.ppermute(images[other], "freq", swap)
    total = sums[0]
    for ahead in range(1, freqs // cores):
        along = [(i, (i + ahead * cores) % freqs) for i in range(freqs)]
        total = total + lax.ppermute(sums[ahead], "freq", along)
    return fields, total


def solution(mesh):
    placed = (
        P(None, "tile", "freq"),
        P("shots"),
        P(None, "freq", "shots"),
        P("shots"),
        P(None, "freq", "shots"),
    )
    return jax.shard_map(
        body,
        mesh=mesh,
        in_specs=placed,
        out_specs=(P("shots", "freq", None, "tile", None), P("shots", "tile", "freq")),
        check_vma=False,
    )
```

```python
import functools

import jax
import jax.numpy as jnp
from jax import lax
from jax.experimental import pallas as pl
from jax.experimental.pallas import tpu as pltpu
from jax.sharding import PartitionSpec as P

PASSES = 5
LANES = 128
SUB = 8
CHUNK = 1024
UNROLL = 4
EARLY = 4
BLOCK = 256

term_weights = (0.3, 0.25, -0.15, 0.12, -0.1, 0.08)
phase_unit = 0.25
slowest = 1.5


def round_up(value, unit):
    return -(-value // unit) * unit


def inject_kernel(rows, halo, row_count, spans, *refs):
    points = [refs[2 * job : 2 * job + 2] for job in range(len(spans))]
    extra_ref, *outs = refs[2 * len(spans) :]
    blocks = outs[0].shape[1] // 2
    pair = 2 * LANES
    cols = blocks * pair
    high_count = blocks * rows
    tall = 2 * SUB
    first = lax.axis_index("tile") * row_count - halo
    size = min(BLOCK, max(high_count, pair))
    ids = lax.broadcasted_iota(jnp.int32, (size, LANES), 0).astype(jnp.float32).astype(jnp.bfloat16)

    def spread(values, line, count):
        one = jnp.broadcast_to(values[line : line + 1], (tall, LANES)).astype(jnp.bfloat16)
        return jnp.concatenate([one] * (count // tall), axis=0)

    def one_hot(index, line, count):
        return jnp.maximum(1.0 - jnp.abs(ids[:count] - spread(index, line, count)), 0.0)

    def add(cell_ref, wave_ref, out_ref, index):
        lines = CHUNK // LANES
        lefts, rights = [], []
        for group in range(0, lines, SUB):
            height = min(SUB, lines)
            at = pl.ds(pl.multiple_of(index * lines + group, height), height)
            cell = cell_ref[at, :]
            row = cell // cols - first
            col = cell % cols
            high = jnp.where((row >= 0) & (row < rows), col // pair * rows + row, -1)
            low = ((col % 2) * LANES + col % pair // 2).astype(jnp.float32)
            pieces = []
            for part in range(2):
                value = wave_ref[part, at, :]
                top = value.astype(jnp.bfloat16).astype(jnp.float32)
                pieces += [top, value - top]
            for line in range(height):
                rights.append(one_hot(low, line, pair))
                variants = [[] for _ in pieces]
                for base in range(0, high_count, size):
                    count = min(size, high_count - base)
                    match = one_hot((high - base).astype(jnp.float32), line, count)
                    for variant, piece in zip(variants, pieces):
                        variant.append(match * spread(piece, line, count))
                lefts.append(jnp.concatenate(sum(variants, []), axis=0))
        total = lax.dot_general(
            jnp.concatenate(lefts, axis=1),
            jnp.concatenate(rights, axis=1),
            (((1,), (1,)), ((), ())),
            preferred_element_type=jnp.float32,
        )
        for part in range(2):
            at = 2 * part * high_count
            both = total[at : at + high_count] + total[at + high_count : at + 2 * high_count]
            for odd in range(2):
                out_at = slice(odd * blocks, (odd + 1) * blocks)
                out_ref[part, out_at] = out_ref[part, out_at] + both[:, odd * LANES : (odd + 1) * LANES].reshape(
                    blocks, rows, LANES
                )

    def run(job, out_ref):
        begin, end = spans[job]
        unroll = next(u for u in (UNROLL, 2, 1) if (end - begin) % u == 0)

        def some_chunks(index, carry):
            for one in range(unroll):
                add(*points[job], out_ref, begin + index * unroll + one)
            return carry

        lax.fori_loop(0, (end - begin) // unroll, some_chunks, 0)

    if len(spans) == 1:
        outs[0][...] = extra_ref[...]
        run(0, outs[0])
        return
    *outs, moved_ref, sem = outs
    move = pltpu.make_async_copy(extra_ref, moved_ref, sem)
    move.start()
    for job, out_ref in enumerate(outs):
        out_ref[...] = jnp.zeros_like(out_ref)
        run(job, out_ref)
    move.wait()


def inject(jobs, extra, rows, halo, row_count, cols):
    whole = pl.BlockSpec(memory_space=pltpu.VMEM)
    alone = len(jobs) == 1
    operands = []
    for cells, waves, _, _ in jobs:
        lines = cells.shape[0] // LANES
        operands += [cells.reshape(lines, LANES), waves.reshape(2, lines, LANES)]
    total = sum(end - begin for *_, begin, end in jobs) * CHUNK
    planes = pltpu.VMEM((2, cols // LANES, rows, LANES), jnp.float32)
    outs = [planes] * len(jobs) + ([] if alone else [pltpu.VMEM(extra.shape, extra.dtype)])
    return pl.pallas_call(
        functools.partial(inject_kernel, rows, halo, row_count, [job[2:] for job in jobs]),
        out_shape=outs,
        in_specs=[whole] * len(operands) + [whole if alone else pl.BlockSpec(memory_space=pltpu.HBM)],
        out_specs=[whole] * len(outs),
        scratch_shapes=[] if alone else [pltpu.SemaphoreType.DMA(())],
        cost_estimate=pl.CostEstimate(
            flops=8 * rows * cols * total, bytes_accessed=12 * total, transcendentals=0
        ),
        name="inject",
    )(*operands, pltpu.with_memory_space_constraint(extra, pltpu.VMEM) if alone else extra)


def sine(angle, square, terms):
    total = None
    for k in range(terms - 1, 0, -1):
        coef = 1.0
        for m in range(2, 2 * k + 2):
            coef /= m
        coef = coef if k % 2 == 0 else -coef
        total = coef if total is None else total * square + coef
    return angle * (total * square + 1.0)


def cosine(square, terms):
    total = None
    for k in range(terms - 1, 0, -1):
        coef = 1.0
        for m in range(2, 2 * k + 1):
            coef /= m
        coef = coef if k % 2 == 0 else -coef
        total = coef if total is None else total * square + coef
    return total * square + 1.0


def terms_for(largest, offset):
    count, size = 1, largest * largest / ((1 + offset) * (2 + offset))
    while size > 3e-8 or count < 2:
        count += 1
        size *= largest * largest / ((2 * count - 1 + offset) * (2 * count + offset))
    return count


def times(a, b):
    return a[0] * b[0] - a[1] * b[1], a[0] * b[1] + a[1] * b[0]


def squared(a):
    twice = a[1] + a[1]
    return 1.0 - twice * a[1], twice * a[0]


def coefficients(speed, number, limit):
    slow = (0.2 * phase_unit) * number / jnp.maximum(speed, 1.0)
    square = slow * slow
    sines, cosines = terms_for(0.2 * limit, 1), terms_for(0.2 * limit, 0)
    a20 = (cosine(square, cosines), sine(slow, square, sines))
    small, square = slow * 0.75, square * 0.5625
    a15 = (cosine(square, cosines), sine(small, square, sines))
    a30 = squared(a15)
    a45 = times(a30, a15)
    a60 = squared(a30)
    a80 = times(a60, a20)
    a100 = times(a80, a20)
    angles = (a100, a80, a60, a45, a30, a20)
    return [(weight * a[0], weight * a[1]) for weight, a in zip(term_weights, angles)]


def depth_kernel(sizes, *refs):
    row_count, steps, halo, vel_halo = sizes
    freqs = lax.axis_size("freq")
    tiles = lax.axis_size("tile")
    pieces, (before_ref, after_ref, src_ref, rec_ref) = refs[:freqs], refs[freqs : freqs + 4]
    fields_ref, *image_refs, terms, sums, speed, flat = refs[freqs + 4 :]
    me = lax.axis_index("freq")
    tile = lax.axis_index("tile")
    number = (me + 1).astype(jnp.float32)
    limit = freqs * phase_unit / slowest
    rows = row_count + 2 * halo
    parts = src_ref.shape[1]
    blocks = parts // 2
    width = pieces[0].shape[-1]
    per_owner = width // LANES

    for back, piece in enumerate(pieces):
        owner = lax.rem(me + freqs - back, freqs)
        for part in range(per_owner):
            lanes = slice(part * LANES, (part + 1) * LANES)
            to = owner * per_owner + part
            for step in range(steps):
                low = vel_halo + row_count
                speed[step, to, :vel_halo, :] = before_ref[back, step, :, lanes]
                speed[step, to, vel_halo:low, :] = piece[step, :, lanes]
                speed[step, to, low : low + vel_halo, :] = after_ref[back, step, :, lanes]

    shape = (SUB, LANES)
    lane = lax.broadcasted_iota(jnp.int32, shape, 1)
    sub = lax.broadcasted_iota(jnp.int32, shape, 0)
    first_lane, last_lane = lane == 0, lane == LANES - 1
    zero = jnp.zeros(shape, jnp.float32)
    edges = (
        (halo - 1, jnp.where(tile == 0, 0.0, 1.0)),
        (halo + row_count, jnp.where(tile == tiles - 1, 0.0, 1.0)),
    )

    def strided(low, count, index=0):
        return pl.ds(low + index, SUB, stride=count)

    def take(value, index):
        return jnp.take_along_axis(value, index, axis=1, mode="promise_in_bounds")

    def split(low, high):
        index = (2 * lane) % LANES
        return [
            jnp.where(lane < LANES // 2, take(low, index + odd), take(high, index + odd)) for odd in range(2)
        ]

    def join(even, odd):
        index = lane // 2
        return [
            jnp.where(lane % 2 == 1, take(odd, index + at), take(even, index + at)) for at in (0, LANES // 2)
        ]

    def share(low, high):
        count = -(-(high - low) // SUB)
        return count + (count % SUB == 0)

    def one_pass(plane, order, low, high):
        count = share(low, high)
        keeps = {}
        for row, keep in edges:
            at, index = divmod(row - low, count)
            if 0 <= at < SUB:
                keeps.setdefault(index, []).append(jnp.where(sub == at, keep, 1.0))

        def load(part, index):
            return terms[order - 1, plane, part, strided(low, count, index), :]

        here = [load(part, 0) for part in range(parts)]
        pair = [load(part, -1) + here[part] for part in range(parts)]
        for index in range(count):
            below = [load(part, index + 1) for part in range(parts)]
            next_pair = [here[part] + below[part] for part in range(parts)]
            stacked = [pair[part] + next_pair[part] for part in range(parts)]
            moved = [pltpu.roll(v, LANES - 1 if part < blocks else 1, 1) for part, v in enumerate(stacked)]
            for part in range(parts):
                blk = part % blocks
                even, odd = stacked[blk], stacked[blocks + blk]
                if part < blocks:
                    other = moved[part + blocks - 1] if blk > 0 else zero
                    side = jnp.where(first_lane, other, moved[part + blocks])
                    total = (even + odd) + even + side
                else:
                    other = moved[blk + 1] if blk + 1 < blocks else zero
                    side = jnp.where(last_lane, other, moved[blk])
                    total = (even + odd) + odd + side
                at = strided(low, count, index)
                if order == 1:
                    total = 0.125 * total
                else:
                    total = 0.25 * total - sums[plane, part, at, :]
                new = total - here[part]
                for keep in keeps.get(index, []):
                    new = new * keep
                    total = total * keep
                if order < PASSES:
                    sums[plane, part, at, :] = total
                terms[order, plane, part, at, :] = new
            here, pair = below, next_pair

    for field, ref in enumerate((src_ref, rec_ref)):
        for part in range(2):
            terms[0, 2 * field + part, :, :rows, :] = ref[part]

    def put(slot, blk, at, pair):
        for half, value in enumerate(join(*pair)):
            flat[slot, 2 * blk + half, at, :] = value

    for step in range(steps):

        def passes(plane, carry):
            for order in range(1, PASSES + 1):
                one_pass(plane, order, PASSES * step + order, rows - PASSES * step - order)
            return carry

        lax.fori_loop(0, 4, passes, 0)
        low, high = PASSES * (step + 1), rows - PASSES * (step + 1)
        count = share(low, high)
        last = step == steps - 1

        def blend(index, carry):
            at = strided(low, count, index)
            vel_at = strided(low - halo + vel_halo, count, index)
            for blk in range(blocks):
                done = []
                speeds = split(*[speed[step, 2 * blk + half, vel_at, :] for half in range(2)])
                for odd in range(2):
                    part = odd * blocks + blk
                    coefs = coefficients(speeds[odd], number, limit)
                    results = []
                    for field in range(2):
                        real, imag = [], []
                        for order, (cr, ci) in enumerate(coefs):
                            tr = terms[order, 2 * field, part, at, :]
                            ti = terms[order, 2 * field + 1, part, at, :]
                            if field == 0:
                                real += [cr * tr - ci * ti]
                                imag += [cr * ti + ci * tr]
                            else:
                                real += [cr * tr + ci * ti]
                                imag += [cr * ti - ci * tr]
                        results += [sum(real[1:], real[0]), sum(imag[1:], imag[0])]
                    if last:
                        results.append(results[0] * results[2] + results[1] * results[3])
                    else:
                        for plane in range(4):
                            terms[0, plane, part, at, :] = results[plane]
                    done.append(results)
                if last:
                    out_at = strided(0, count, index)
                    for slot, pair in zip((0, 1, 2, 3, 4 + step), zip(*done)):
                        put(slot, blk, out_at, pair)
            return carry

        lax.fori_loop(0, count, blend, 0)
        if not last:
            image_count = row_count // SUB

            def correlate(index, carry):
                for blk in range(blocks):
                    pair = []
                    for odd in range(2):
                        field = [
                            terms[0, plane, odd * blocks + blk, strided(halo, image_count, index), :]
                            for plane in range(4)
                        ]
                        pair.append(field[0] * field[2] + field[1] * field[3])
                    put(4 + step, blk, strided(0, image_count, index), pair)
                return carry

            lax.fori_loop(0, image_count, correlate, 0)

        for other, ref in enumerate(image_refs):
            cores, places = len(image_refs), ref.shape[0]
            core, place = lax.rem(me, cores), lax.div(me, cores)
            for ahead in range(places):
                owner = lax.rem(place + ahead, places) * cores + lax.rem(core + other, cores)
                for part in range(per_owner):
                    lanes = slice(part * LANES, (part + 1) * LANES)
                    ref[ahead, step, :, lanes] = flat[4 + step, owner * per_owner + part]
    for plane in range(4):
        for part in range(parts):
            lanes = slice(part * LANES, (part + 1) * LANES)
            fields_ref[plane // 2, 0, plane % 2, :, lanes] = flat[plane, part]


def depth_steps(pieces, before, after, src, rec, sizes):
    row_count, steps, halo, vel_halo = sizes
    width = pieces[0].shape[-1]
    owners = len(pieces)
    rows = row_count + 2 * halo
    parts = owners * width // LANES
    tall = row_count + 2 * vel_halo
    whole = pl.BlockSpec(memory_space=pltpu.VMEM)
    cores = cores_of(owners)
    return pl.pallas_call(
        functools.partial(depth_kernel, sizes),
        out_shape=(
            pltpu.VMEM((2, 1, 2, row_count, owners * width), jnp.float32),
            *[pltpu.VMEM((owners // cores, steps, row_count, width), jnp.float32)] * cores,
        ),
        in_specs=[whole] * (owners + 4),
        out_specs=(whole,) * (cores + 1),
        scratch_shapes=[
            pltpu.VMEM((PASSES + 1, 4, parts, rows + 2 * SUB, LANES), jnp.float32),
            pltpu.VMEM((4, parts, rows + 2 * SUB, LANES), jnp.float32),
            pltpu.VMEM((steps, parts, tall + 2 * SUB, LANES), jnp.float32),
            pltpu.VMEM((4 + steps, parts, row_count, LANES), jnp.float32),
        ],
        cost_estimate=pl.CostEstimate(
            flops=steps * 300 * rows * owners * width, bytes_accessed=64 * rows * owners * width, transcendentals=0
        ),
        name="depth",
        compiler_params=pltpu.CompilerParams(),
    )(*[pltpu.with_memory_space_constraint(one, pltpu.VMEM) for one in (*pieces, before, after, src, rec)])


def cores_of(freqs):
    return 2 - freqs % 2


def shifts(axis):
    count = lax.axis_size(axis)
    return [[(i, (i + k) % count) for i in range(count)] for k in range(1, count)]


def body(velocity, src_cell, src_wave, rec_cell, rec_data):
    steps, row_count, width = velocity.shape
    freqs, tiles = lax.axis_size("freq"), lax.axis_size("tile")
    assert src_cell.shape[0] % CHUNK == 0 and rec_cell.shape[0] % (EARLY * CHUNK) == 0
    assert width % LANES == 0 and width * freqs % (2 * LANES) == 0 and row_count % SUB == 0
    me = lax.axis_index("freq")
    halo = PASSES * steps
    vel_halo = round_up(PASSES * (steps - 1), SUB)
    rows = row_count + 2 * halo
    sizes = (row_count, steps, halo, vel_halo)

    cols = width * freqs
    others = [lax.ppermute(velocity, "freq", pairs) for pairs in shifts("freq")]
    src_chunks, rec_chunks = src_cell.shape[0] // CHUNK, rec_cell.shape[0] // CHUNK
    early = rec_chunks // EARLY
    jobs = [(src_cell, src_wave, 0, src_chunks), (rec_cell, rec_data, 0, early)]
    src, rec, own = inject(jobs, velocity, rows, halo, row_count, cols)
    others, src, own = lax.optimization_barrier((others, src, own))
    pieces = [own] + others
    up = [(i, i + 1) for i in range(tiles - 1)]
    down = [(j, i) for i, j in up]
    lowest = jnp.stack([p[:, row_count - vel_halo :] for p in pieces])
    highest = jnp.stack([p[:, :vel_halo] for p in pieces])
    lowest, highest, rec = lax.optimization_barrier((lowest, highest, rec))
    before = lax.ppermute(lowest, "tile", up)
    after = lax.ppermute(highest, "tile", down)
    (rec,) = inject([(rec_cell, rec_data, early, rec_chunks)], rec, rows, halo, row_count, cols)
    fields, *images = depth_steps(pieces, before, after, src, rec, sizes)
    cores = cores_of(freqs)
    sums = images[0]
    for other in range(1, cores):
        swap = [(i, i - i % cores + (i + other) % cores) for i in range(freqs)]
        sums = sums + lax.ppermute(images[other], "freq", swap)
    total = sums[0]
    for ahead in range(1, freqs // cores):
        along = [(i, (i + ahead * cores) % freqs) for i in range(freqs)]
        total = total + lax.ppermute(sums[ahead], "freq", along)
    return fields, total


def solution(mesh):
    placed = (
        P(None, "tile", "freq"),
        P("shots"),
        P(None, "freq", "shots"),
        P("shots"),
        P(None, "freq", "shots"),
    )
    return jax.shard_map(
        body,
        mesh=mesh,
        in_specs=placed,
        out_specs=(P("shots", "freq", None, "tile", None), P("shots", "tile", "freq")),
        check_vma=False,
    )
```

```python
import functools

import jax
import jax.numpy as jnp
from jax import lax
from jax.experimental import pallas as pl
from jax.experimental.pallas import tpu as pltpu
from jax.sharding import PartitionSpec as P

PASSES = 5
LANES = 128
SUB = 8
CHUNK = 1024
UNROLL = 4
EARLY = 4
BLOCK = 256

term_weights = (0.3, 0.25, -0.15, 0.12, -0.1, 0.08)
phase_unit = 0.25
slowest = 1.5


def round_up(value, unit):
    return -(-value // unit) * unit


def inject_kernel(rows, halo, row_count, spans, *refs):
    points = [refs[2 * job : 2 * job + 2] for job in range(len(spans))]
    extra_ref, *outs = refs[2 * len(spans) :]
    blocks = outs[0].shape[1] // 2
    pair = 2 * LANES
    cols = blocks * pair
    high_count = blocks * rows
    tall = 2 * SUB
    first = lax.axis_index("tile") * row_count - halo
    size = min(BLOCK, max(high_count, pair))
    ids = lax.broadcasted_iota(jnp.int32, (size, LANES), 0).astype(jnp.float32).astype(jnp.bfloat16)

    def spread(values, line, count):
        one = jnp.broadcast_to(values[line : line + 1], (tall, LANES)).astype(jnp.bfloat16)
        return jnp.concatenate([one] * (count // tall), axis=0)

    def one_hot(index, line, count):
        return jnp.maximum(1.0 - jnp.abs(ids[:count] - spread(index, line, count)), 0.0)

    def add(cell_ref, wave_ref, out_ref, index):
        lines = CHUNK // LANES
        lefts, rights = [], []
        for group in range(0, lines, SUB):
            height = min(SUB, lines)
            at = pl.ds(pl.multiple_of(index * lines + group, height), height)
            cell = cell_ref[at, :]
            row = cell // cols - first
            col = cell % cols
            high = jnp.where((row >= 0) & (row < rows), col // pair * rows + row, -1)
            low = ((col % 2) * LANES + col % pair // 2).astype(jnp.float32)
            pieces = []
            for part in range(2):
                value = wave_ref[part, at, :]
                top = value.astype(jnp.bfloat16).astype(jnp.float32)
                pieces += [top, value - top]
            for line in range(height):
                rights.append(one_hot(low, line, pair))
                variants = [[] for _ in pieces]
                for base in range(0, high_count, size):
                    count = min(size, high_count - base)
                    match = one_hot((high - base).astype(jnp.float32), line, count)
                    for variant, piece in zip(variants, pieces):
                        variant.append(match * spread(piece, line, count))
                lefts.append(jnp.concatenate(sum(variants, []), axis=0))
        total = lax.dot_general(
            jnp.concatenate(lefts, axis=1),
            jnp.concatenate(rights, axis=1),
            (((1,), (1,)), ((), ())),
            preferred_element_type=jnp.float32,
        )
        for part in range(2):
            at = 2 * part * high_count
            both = total[at : at + high_count] + total[at + high_count : at + 2 * high_count]
            for odd in range(2):
                out_at = slice(odd * blocks, (odd + 1) * blocks)
                out_ref[part, out_at] = out_ref[part, out_at] + both[:, odd * LANES : (odd + 1) * LANES].reshape(
                    blocks, rows, LANES
                )

    def run(job, out_ref):
        begin, end = spans[job]
        unroll = next(u for u in (UNROLL, 2, 1) if (end - begin) % u == 0)

        def some_chunks(index, carry):
            for one in range(unroll):
                add(*points[job], out_ref, begin + index * unroll + one)
            return carry

        lax.fori_loop(0, (end - begin) // unroll, some_chunks, 0)

    if len(spans) == 1:
        outs[0][...] = extra_ref[...]
        run(0, outs[0])
        return
    *outs, moved_ref, sem = outs
    move = pltpu.make_async_copy(extra_ref, moved_ref, sem)
    move.start()
    for job, out_ref in enumerate(outs):
        out_ref[...] = jnp.zeros_like(out_ref)
        run(job, out_ref)
    move.wait()


def inject(jobs, extra, rows, halo, row_count, cols):
    whole = pl.BlockSpec(memory_space=pltpu.VMEM)
    alone = len(jobs) == 1
    operands = []
    for cells, waves, _, _ in jobs:
        lines = cells.shape[0] // LANES
        operands += [cells.reshape(lines, LANES), waves.reshape(2, lines, LANES)]
    total = sum(end - begin for *_, begin, end in jobs) * CHUNK
    planes = pltpu.VMEM((2, cols // LANES, rows, LANES), jnp.float32)
    outs = [planes] * len(jobs) + ([] if alone else [pltpu.VMEM(extra.shape, extra.dtype)])
    return pl.pallas_call(
        functools.partial(inject_kernel, rows, halo, row_count, [job[2:] for job in jobs]),
        out_shape=outs,
        in_specs=[whole] * len(operands) + [whole if alone else pl.BlockSpec(memory_space=pltpu.HBM)],
        out_specs=[whole] * len(outs),
        scratch_shapes=[] if alone else [pltpu.SemaphoreType.DMA(())],
        cost_estimate=pl.CostEstimate(
            flops=8 * rows * cols * total, bytes_accessed=12 * total, transcendentals=0
        ),
        name="inject",
    )(*operands, pltpu.with_memory_space_constraint(extra, pltpu.VMEM) if alone else extra)


def sine(angle, square, terms):
    total = None
    for k in range(terms - 1, 0, -1):
        coef = 1.0
        for m in range(2, 2 * k + 2):
            coef /= m
        coef = coef if k % 2 == 0 else -coef
        total = coef if total is None else total * square + coef
    return angle * (total * square + 1.0)


def cosine(square, terms):
    total = None
    for k in range(terms - 1, 0, -1):
        coef = 1.0
        for m in range(2, 2 * k + 1):
            coef /= m
        coef = coef if k % 2 == 0 else -coef
        total = coef if total is None else total * square + coef
    return total * square + 1.0


def terms_for(largest, offset):
    count, size = 1, largest * largest / ((1 + offset) * (2 + offset))
    while size > 3e-8 or count < 2:
        count += 1
        size *= largest * largest / ((2 * count - 1 + offset) * (2 * count + offset))
    return count


def times(a, b):
    return a[0] * b[0] - a[1] * b[1], a[0] * b[1] + a[1] * b[0]


def squared(a):
    twice = a[1] + a[1]
    return 1.0 - twice * a[1], twice * a[0]


def onward(a, before, twice):
    return twice * a[0] - before[0], twice * a[1] - before[1]


def coefficients(speed, number, limit):
    slow = (0.2 * phase_unit) * number / jnp.maximum(speed, 1.0)
    square = slow * slow
    sines, cosines = terms_for(0.2 * limit, 1), terms_for(0.2 * limit, 0)
    a20 = (cosine(square, cosines), sine(slow, square, sines))
    small, square = slow * 0.75, square * 0.5625
    a15 = (cosine(square, cosines), sine(small, square, sines))
    a30 = squared(a15)
    a45 = onward(a30, a15, a15[0] + a15[0])
    a60 = squared(a30)
    a80 = times(a60, a20)
    a100 = onward(a80, a60, a20[0] + a20[0])
    angles = (a100, a80, a60, a45, a30, a20)
    return [(weight * a[0], weight * a[1]) for weight, a in zip(term_weights, angles)]


def depth_kernel(sizes, *refs):
    row_count, steps, halo, vel_halo = sizes
    freqs = lax.axis_size("freq")
    tiles = lax.axis_size("tile")
    pieces, (before_ref, after_ref, src_ref, rec_ref) = refs[:freqs], refs[freqs : freqs + 4]
    fields_ref, *image_refs, terms, sums, speed, flat = refs[freqs + 4 :]
    me = lax.axis_index("freq")
    tile = lax.axis_index("tile")
    number = (me + 1).astype(jnp.float32)
    limit = freqs * phase_unit / slowest
    rows = row_count + 2 * halo
    parts = src_ref.shape[1]
    blocks = parts // 2
    width = pieces[0].shape[-1]
    per_owner = width // LANES

    for back, piece in enumerate(pieces):
        owner = lax.rem(me + freqs - back, freqs)
        for part in range(per_owner):
            lanes = slice(part * LANES, (part + 1) * LANES)
            to = owner * per_owner + part
            for step in range(steps):
                low = vel_halo + row_count
                speed[step, to, :vel_halo, :] = before_ref[back, step, :, lanes]
                speed[step, to, vel_halo:low, :] = piece[step, :, lanes]
                speed[step, to, low : low + vel_halo, :] = after_ref[back, step, :, lanes]

    shape = (SUB, LANES)
    lane = lax.broadcasted_iota(jnp.int32, shape, 1)
    sub = lax.broadcasted_iota(jnp.int32, shape, 0)
    first_lane, last_lane = lane == 0, lane == LANES - 1
    zero = jnp.zeros(shape, jnp.float32)
    edges = (
        (halo - 1, jnp.where(tile == 0, 0.0, 1.0)),
        (halo + row_count, jnp.where(tile == tiles - 1, 0.0, 1.0)),
    )

    def strided(low, count, index=0):
        return pl.ds(low + index, SUB, stride=count)

    def take(value, index):
        return jnp.take_along_axis(value, index, axis=1, mode="promise_in_bounds")

    def split(low, high):
        index = (2 * lane) % LANES
        return [
            jnp.where(lane < LANES // 2, take(low, index + odd), take(high, index + odd)) for odd in range(2)
        ]

    def join(even, odd):
        index = lane // 2
        return [
            jnp.where(lane % 2 == 1, take(odd, index + at), take(even, index + at)) for at in (0, LANES // 2)
        ]

    def share(low, high):
        count = -(-(high - low) // SUB)
        return count + (count % SUB == 0)

    def one_pass(plane, order, low, high):
        count = share(low, high)
        keeps = {}
        for row, keep in edges:
            at, index = divmod(row - low, count)
            if 0 <= at < SUB:
                keeps.setdefault(index, []).append(jnp.where(sub == at, keep, 1.0))

        def load(part, index):
            return terms[order - 1, plane, part, strided(low, count, index), :]

        here = [load(part, 0) for part in range(parts)]
        pair = [load(part, -1) + here[part] for part in range(parts)]
        for index in range(count):
            below = [load(part, index + 1) for part in range(parts)]
            next_pair = [here[part] + below[part] for part in range(parts)]
            stacked = [pair[part] + next_pair[part] for part in range(parts)]
            moved = [pltpu.roll(v, LANES - 1 if part < blocks else 1, 1) for part, v in enumerate(stacked)]
            for part in range(parts):
                blk = part % blocks
                even, odd = stacked[blk], stacked[blocks + blk]
                if part < blocks:
                    other = moved[part + blocks - 1] if blk > 0 else zero
                    side = jnp.where(first_lane, other, moved[part + blocks])
                    total = (even + odd) + even + side
                else:
                    other = moved[blk + 1] if blk + 1 < blocks else zero
                    side = jnp.where(last_lane, other, moved[blk])
                    total = (even + odd) + odd + side
                at = strided(low, count, index)
                if order == 1:
                    total = 0.125 * total
                else:
                    total = 0.25 * total - sums[plane, part, at, :]
                new = total - here[part]
                for keep in keeps.get(index, []):
                    new = new * keep
                    total = total * keep
                if order < PASSES:
                    sums[plane, part, at, :] = total
                terms[order, plane, part, at, :] = new
            here, pair = below, next_pair

    for field, ref in enumerate((src_ref, rec_ref)):
        for part in range(2):
            terms[0, 2 * field + part, :, :rows, :] = ref[part]

    def put(slot, blk, at, pair):
        for half, value in enumerate(join(*pair)):
            flat[slot, 2 * blk + half, at, :] = value

    for step in range(steps):

        def passes(plane, carry):
            for order in range(1, PASSES + 1):
                one_pass(plane, order, PASSES * step + order, rows - PASSES * step - order)
            return carry

        lax.fori_loop(0, 4, passes, 0)
        low, high = PASSES * (step + 1), rows - PASSES * (step + 1)
        count = share(low, high)
        last = step == steps - 1

        def blend(index, carry):
            at = strided(low, count, index)
            vel_at = strided(low - halo + vel_halo, count, index)
            for blk in range(blocks):
                done = []
                speeds = split(*[speed[step, 2 * blk + half, vel_at, :] for half in range(2)])
                for odd in range(2):
                    part = odd * blocks + blk
                    coefs = coefficients(speeds[odd], number, limit)
                    results = []
                    for field in range(2):
                        real, imag = [], []
                        for order, (cr, ci) in enumerate(coefs):
                            tr = terms[order, 2 * field, part, at, :]
                            ti = terms[order, 2 * field + 1, part, at, :]
                            if field == 0:
                                real += [cr * tr - ci * ti]
                                imag += [cr * ti + ci * tr]
                            else:
                                real += [cr * tr + ci * ti]
                                imag += [cr * ti - ci * tr]
                        results += [sum(real[1:], real[0]), sum(imag[1:], imag[0])]
                    if last:
                        results.append(results[0] * results[2] + results[1] * results[3])
                    else:
                        for plane in range(4):
                            terms[0, plane, part, at, :] = results[plane]
                    done.append(results)
                if last:
                    out_at = strided(0, count, index)
                    for slot, pair in zip((0, 1, 2, 3, 4 + step), zip(*done)):
                        put(slot, blk, out_at, pair)
            return carry

        lax.fori_loop(0, count, blend, 0)
        if not last:
            image_count = row_count // SUB

            def correlate(index, carry):
                for blk in range(blocks):
                    pair = []
                    for odd in range(2):
                        field = [
                            terms[0, plane, odd * blocks + blk, strided(halo, image_count, index), :]
                            for plane in range(4)
                        ]
                        pair.append(field[0] * field[2] + field[1] * field[3])
                    put(4 + step, blk, strided(0, image_count, index), pair)
                return carry

            lax.fori_loop(0, image_count, correlate, 0)

        for other, ref in enumerate(image_refs):
            cores, places = len(image_refs), ref.shape[0]
            core, place = lax.rem(me, cores), lax.div(me, cores)
            for ahead in range(places):
                owner = lax.rem(place + ahead, places) * cores + lax.rem(core + other, cores)
                for part in range(per_owner):
                    lanes = slice(part * LANES, (part + 1) * LANES)
                    ref[ahead, step, :, lanes] = flat[4 + step, owner * per_owner + part]
    for plane in range(4):
        for part in range(parts):
            lanes = slice(part * LANES, (part + 1) * LANES)
            fields_ref[plane // 2, 0, plane % 2, :, lanes] = flat[plane, part]


def depth_steps(pieces, before, after, src, rec, sizes):
    row_count, steps, halo, vel_halo = sizes
    width = pieces[0].shape[-1]
    owners = len(pieces)
    rows = row_count + 2 * halo
    parts = owners * width // LANES
    tall = row_count + 2 * vel_halo
    whole = pl.BlockSpec(memory_space=pltpu.VMEM)
    cores = cores_of(owners)
    return pl.pallas_call(
        functools.partial(depth_kernel, sizes),
        out_shape=(
            pltpu.VMEM((2, 1, 2, row_count, owners * width), jnp.float32),
            *[pltpu.VMEM((owners // cores, steps, row_count, width), jnp.float32)] * cores,
        ),
        in_specs=[whole] * (owners + 4),
        out_specs=(whole,) * (cores + 1),
        scratch_shapes=[
            pltpu.VMEM((PASSES + 1, 4, parts, rows + 2 * SUB, LANES), jnp.float32),
            pltpu.VMEM((4, parts, rows + 2 * SUB, LANES), jnp.float32),
            pltpu.VMEM((steps, parts, tall + 2 * SUB, LANES), jnp.float32),
            pltpu.VMEM((4 + steps, parts, row_count, LANES), jnp.float32),
        ],
        cost_estimate=pl.CostEstimate(
            flops=steps * 300 * rows * owners * width, bytes_accessed=64 * rows * owners * width, transcendentals=0
        ),
        name="depth",
        compiler_params=pltpu.CompilerParams(),
    )(*[pltpu.with_memory_space_constraint(one, pltpu.VMEM) for one in (*pieces, before, after, src, rec)])


def cores_of(freqs):
    return 2 - freqs % 2


def shifts(axis):
    count = lax.axis_size(axis)
    return [[(i, (i + k) % count) for i in range(count)] for k in range(1, count)]


def body(velocity, src_cell, src_wave, rec_cell, rec_data):
    steps, row_count, width = velocity.shape
    freqs, tiles = lax.axis_size("freq"), lax.axis_size("tile")
    assert src_cell.shape[0] % CHUNK == 0 and rec_cell.shape[0] % (EARLY * CHUNK) == 0
    assert width % LANES == 0 and width * freqs % (2 * LANES) == 0 and row_count % SUB == 0
    me = lax.axis_index("freq")
    halo = PASSES * steps
    vel_halo = round_up(PASSES * (steps - 1), SUB)
    rows = row_count + 2 * halo
    sizes = (row_count, steps, halo, vel_halo)

    cols = width * freqs
    others = [lax.ppermute(velocity, "freq", pairs) for pairs in shifts("freq")]
    src_chunks, rec_chunks = src_cell.shape[0] // CHUNK, rec_cell.shape[0] // CHUNK
    early = rec_chunks // EARLY
    jobs = [(src_cell, src_wave, 0, src_chunks), (rec_cell, rec_data, 0, early)]
    src, rec, own = inject(jobs, velocity, rows, halo, row_count, cols)
    others, src, own = lax.optimization_barrier((others, src, own))
    pieces = [own] + others
    up = [(i, i + 1) for i in range(tiles - 1)]
    down = [(j, i) for i, j in up]
    lowest = jnp.stack([p[:, row_count - vel_halo :] for p in pieces])
    highest = jnp.stack([p[:, :vel_halo] for p in pieces])
    lowest, highest, rec = lax.optimization_barrier((lowest, highest, rec))
    before = lax.ppermute(lowest, "tile", up)
    after = lax.ppermute(highest, "tile", down)
    (rec,) = inject([(rec_cell, rec_data, early, rec_chunks)], rec, rows, halo, row_count, cols)
    fields, *images = depth_steps(pieces, before, after, src, rec, sizes)
    cores = cores_of(freqs)
    sums = images[0]
    for other in range(1, cores):
        swap = [(i, i - i % cores + (i + other) % cores) for i in range(freqs)]
        sums = sums + lax.ppermute(images[other], "freq", swap)
    total = sums[0]
    for ahead in range(1, freqs // cores):
        along = [(i, (i + ahead * cores) % freqs) for i in range(freqs)]
        total = total + lax.ppermute(sums[ahead], "freq", along)
    return fields, total


def solution(mesh):
    placed = (
        P(None, "tile", "freq"),
        P("shots"),
        P(None, "freq", "shots"),
        P("shots"),
        P(None, "freq", "shots"),
    )
    return jax.shard_map(
        body,
        mesh=mesh,
        in_specs=placed,
        out_specs=(P("shots", "freq", None, "tile", None), P("shots", "tile", "freq")),
        check_vma=False,
    )
```
